256 devices in a mesh: frame: 64 (over y, x_hi, z), clip: 4 (over x_lo, core).
Axes of the slice: x: 4 (x_hi: 2, x_lo: 2; x = x_hi * 2 + x_lo), y: 4, z: 8, core: 2. Of those that a mesh axis runs over, the one named last changes fastest.
Arguments:
- tokens: bfloat16 [4, 512, 2, 49, 256], P('clip', 'frame'), may hold values from -6 to 6
- lengths: int32 [4], P('clip'), may hold values from 256 to 512, as said below
- norm_gain: float32 [256], replicated, may hold values from 0.25 to 1.75
- norm_bias: float32 [256], replicated, may hold values from -1.5 to 1.5
- qkv_weight: float32 [256, 768], replicated, may hold values from -0.375 to 0.375
- qkv_bias: float32 [768], replicated, may hold values from -1.5 to 1.5
- proj_weight: float32 [256, 256], replicated, may hold values from -0.375 to 0.375
- proj_bias: float32 [256], replicated, may hold values from -1.5 to 1.5
- grad_out: bfloat16 [4, 512, 2, 49, 256], P('clip', 'frame'), may hold values from -6 to 6
Outputs:
- mixed: bfloat16 [4, 512, 2, 49, 256], P('clip', 'frame')
- grad_tokens: bfloat16 [4, 512, 2, 49, 256], P('clip', 'frame')
- grad_gain: float32 [256], replicated
- grad_nbias: float32 [256], replicated
- grad_qkv_weight: float32 [256, 768], replicated
- grad_qkv_bias: float32 [768], replicated
- grad_proj_weight: float32 [256, 256], replicated
- grad_proj_bias: float32 [256], replicated
The draws below stay inside these ranges and needn't reach their ends.
Inputs may be any that keep to these rules, and one draw needn't show every extreme that they name: `lengths`: each clip has at least 256 frames that are not padding, and at least one clip has all 512 frames.
All inputs are finite; a program needn't handle non-finite values.
Results may differ from the reference program's by a relative error of at most 0.012.
Values may be sent and summed in bfloat16 or wider, within the bound.
No kernel may reach another device: no remote copies, remote signals or barrier semaphores. Data moves between devices by JAX's collectives and lax.ppermute only.
A program may use at most 192 MiB of HBM per device.

```python
import jax
import jax.numpy as jnp
from jax import lax

D = 256
HEADS = 8
WT = 8
PATCH = 49
WIN_DEV = 2
FRAMES = 512
CLIPS = 4
N_FRAME = 64


def draw_lengths(key, part):
    base_key = jax.random.fold_in(key, 11)
    pick_key = jax.random.fold_in(key, 23)
    base = jax.random.randint(base_key, (CLIPS,), FRAMES // 2, FRAMES + 1, dtype=jnp.int32)
    chosen = jax.random.randint(pick_key, (), 0, CLIPS, dtype=jnp.int32)
    return jnp.where(jnp.arange(CLIPS, dtype=jnp.int32) == chosen, jnp.int32(FRAMES), base).astype(jnp.int32)


def steps_of(stream_key, extent, pieces, smallest, largest):
    def one(dim, blocks):
        heights = jax.random.uniform(jax.random.fold_in(jax.random.fold_in(stream_key, 6), dim), (blocks,), jnp.float32, smallest / len(pieces), largest / len(pieces))
        return jnp.repeat(jnp.exp(heights), extent[dim] // blocks).reshape((-1,) + (1,) * (len(extent) - dim - 1))

    level = one(*pieces[0])
    for cut in pieces[1:]:
        level = level * one(*cut)
    return level


def centred(key, extent, spread, bound, shards=(), kind=jnp.bfloat16):
    gain = steps_of(key, extent, shards, -0.22, 0.18) if shards else 1.0
    array = jax.random.normal(key, extent, jnp.float32) * spread * gain
    return jnp.minimum(jnp.maximum(array, -bound), bound).astype(kind)


def setup_inputs(seed: int = 0) -> dict:
    keys = jax.random.split(jax.random.key(seed), 10)
    tokens = centred(keys[0], (CLIPS, FRAMES, WIN_DEV, PATCH, D), 1.0, 6.0, ((0, 4), (1, 64)))
    lengths = draw_lengths(jax.random.fold_in(keys[9], 71), 0)
    norm_gain = jnp.clip(1.0 + 0.15 * jax.random.normal(keys[2], (D,), jnp.float32), 0.25, 1.75)
    norm_bias = centred(keys[3], (D,), 0.3, 1.5, (), jnp.float32)
    qkv_weight = centred(keys[4], (D, 3 * D), D ** -0.5, 0.375, (), jnp.float32)
    qkv_bias = centred(keys[5], (3 * D,), 0.3, 1.5, (), jnp.float32)
    proj_weight = centred(keys[6], (D, D), D ** -0.5, 0.375, (), jnp.float32)
    proj_bias = centred(keys[7], (D,), 0.3, 1.5, (), jnp.float32)
    grad_out = centred(keys[8], (CLIPS, FRAMES, WIN_DEV, PATCH, D), 1.0, 6.0, ((0, 4), (1, 64)))
    return {"tokens": tokens, "lengths": lengths, "norm_gain": norm_gain, "norm_bias": norm_bias, "qkv_weight": qkv_weight, "qkv_bias": qkv_bias, "proj_weight": proj_weight, "proj_bias": proj_bias, "grad_out": grad_out}


def branch(slab, length, first_frame, frame_total, norm_gain, norm_bias, qkv_weight, qkv_bias, proj_weight, proj_bias):
    frames, windows, patch_len, model_width = slab.shape
    head_count = HEADS
    head_depth = model_width // head_count
    offset = WT // 2
    frame_index = jnp.mod(first_frame + jnp.arange(frames, dtype=jnp.int32), frame_total)
    valid_frame = frame_index < length
    region = frame_index < offset
    values = slab.astype(jnp.float32)
    mean_val = lax.optimization_barrier(jnp.mean(values, axis=-1, keepdims=True))
    variance = lax.optimization_barrier(jnp.mean((values - mean_val) ** 2, axis=-1, keepdims=True))
    normed = ((values - mean_val) * lax.rsqrt(variance + 1e-05) * norm_gain + norm_bias).astype(jnp.bfloat16)
    project_qkv = jnp.dot(normed.reshape(-1, model_width), qkv_weight.astype(jnp.bfloat16), preferred_element_type=jnp.float32) + qkv_bias
    project_qkv = project_qkv.astype(jnp.bfloat16)
    time_windows = frames // WT
    project_qkv = project_qkv.reshape(time_windows, WT, windows, patch_len, 3, head_count, head_depth)
    project_qkv = project_qkv.transpose(4, 0, 2, 5, 1, 3, 6).reshape(3, time_windows, windows, head_count, WT * patch_len, head_depth)
    queries = project_qkv[0].astype(jnp.float32)
    keys_f = project_qkv[1].astype(jnp.float32)
    values_f = project_qkv[2].astype(jnp.float32)
    key_valid = jnp.repeat(valid_frame.reshape(time_windows, WT), patch_len, axis=1)
    key_region = jnp.repeat(region.reshape(time_windows, WT), patch_len, axis=1)
    allowed = key_valid[:, None, :] & (key_region[:, :, None] == key_region[:, None, :])
    scores = jnp.einsum('nwhqe,nwhke->nwhqk', queries, keys_f) * head_depth ** (-0.5)
    scores = jnp.where(allowed[:, None, None], scores, -1000000000.0)
    attn_probs = jax.nn.softmax(scores, axis=-1).astype(jnp.bfloat16)
    attended = jnp.einsum('nwhqk,nwhke->nwhqe', attn_probs.astype(jnp.float32), values_f).astype(jnp.bfloat16)
    attended = attended.reshape(time_windows, windows, head_count, WT, patch_len, head_depth)
    attended = attended.transpose(0, 3, 1, 4, 2, 5).reshape(-1, model_width)
    projected = jnp.dot(attended, proj_weight.astype(jnp.bfloat16), preferred_element_type=jnp.float32) + proj_bias
    projected = projected.reshape(frames, windows, patch_len, model_width) * valid_frame.astype(jnp.float32)[:, None, None, None]
    return projected.astype(jnp.bfloat16)

def reference(tokens, lengths, norm_gain, norm_bias, qkv_weight, qkv_bias, proj_weight, proj_bias, grad_out):
    offset = WT // 2
    params = (norm_gain, norm_bias, qkv_weight, qkv_bias, proj_weight, proj_bias)
    clips = tokens.shape[0]
    frame_total = tokens.shape[1]
    frames_dev = frame_total // N_FRAME
    tail_shape = tokens.shape[2:]
    rolled = jnp.roll(tokens, -offset, axis=1).reshape((clips * N_FRAME, frames_dev) + tail_shape)
    grad_slabs = jnp.roll(grad_out, -offset, axis=1).reshape((clips * N_FRAME, frames_dev) + tail_shape)

    def per_slab(operands):
        slab, grad_slab, slab_index = operands
        clip_index = slab_index // N_FRAME
        frame_slot = slab_index % N_FRAME
        length = lengths[clip_index]
        first_frame = frame_slot * frames_dev + offset

        def local_fn(slab_in, param_set):
            return branch(slab_in, length, first_frame, frame_total, *param_set)
        branch_out, pullback = jax.vjp(local_fn, slab, params)
        grad_rolled, grad_params = pullback(grad_slab)
        return (branch_out, grad_rolled, tuple((g.astype(jnp.float32) for g in grad_params)))
    branch_out, grad_rolled, grad_params = lax.map(per_slab, (rolled, grad_slabs, jnp.arange(clips * N_FRAME, dtype=jnp.int32)))
    summed = tuple((lax.optimization_barrier(jnp.sum(g, axis=0)) for g in grad_params))
    branch_full = jnp.roll(branch_out.reshape(tokens.shape), offset, axis=1)
    grad_back = jnp.roll(grad_rolled.reshape(tokens.shape), offset, axis=1)
    mixed = (tokens.astype(jnp.float32) + branch_full.astype(jnp.float32)).astype(jnp.bfloat16)
    grad_tokens = grad_out + grad_back
    return (mixed, grad_tokens, summed[0], summed[1], summed[2], summed[3], summed[4], summed[5])
```

```python
import functools
import math

import jax
import jax.numpy as jnp
from jax import lax
from jax.experimental import pallas as pl
from jax.experimental.pallas import tpu as pltpu
from jax.sharding import PartitionSpec as P

HEADS = 8
WT = 8
HALF = WT // 2
AXES = ("frame", "clip")
BIG = 2.0**100
EXT = 16
f32, bf16 = jnp.float32, jnp.bfloat16


def passed_along(array, axis, by):
    devices = lax.axis_size(axis)
    return lax.ppermute(array, axis, [(i, (i + by) % devices) for i in range(devices)])


def mm(a, b, ca=1, cb=0):
    return lax.dot_general(a, b, (((ca,), (cb,)), ((), ())), preferred_element_type=f32)


def block_kernel(
    frame_total, sc, tok, gr, halo, gain, nb, w, wT, wp, wpT, bq, bp,
    mixed, gtok, send, pay,
    xs, gs, normT, gN, qkvT, doT, attT, dqT, acc,
):
    frames, windows, patch, width = tok.shape
    rows = WT * patch
    depth = width // HEADS
    scale = depth ** (-0.5)
    length, first = sc[0], sc[1]

    def frame_of(u):
        t = first + u
        return jnp.where(t >= frame_total, t - frame_total, t)

    def valid_of(u):
        return jnp.where(frame_of(u) < length, 1.0, 0.0).astype(f32)

    for win in range(windows):
        for u in range(WT):
            at = pl.ds(u * patch, patch)
            x_u = tok[HALF + u, win] if u < HALF else halo[0, u - HALF, win]
            g_u = gr[HALF + u, win] if u < HALF else halo[1, u - HALF, win]
            xs[win, at, :] = x_u.astype(f32)
            gs[win, at, :] = g_u.astype(f32) * valid_of(u)

    lane = lax.broadcasted_iota(jnp.int32, (EXT, rows), 1)
    row = lax.broadcasted_iota(jnp.int32, (EXT, rows), 0)
    u_lane = jnp.zeros((EXT, rows), jnp.int32)
    for u in range(1, WT):
        u_lane = u_lane + jnp.where(lane >= u * patch, 1, 0)
    t_lane = frame_of(u_lane)
    bad = jnp.where(t_lane < length, 0.0, 1.0)
    reg = jnp.where(t_lane < HALF, 1.0, 0.0)
    q_ext = jnp.where(row == 0, 1.0, jnp.where(row == 1, reg, jnp.where(row == 2, 1.0 - reg, 0.0)))
    k_ext = jnp.where(row == 0, bad, jnp.where(row == 1, 1.0 - reg, jnp.where(row == 2, reg, 0.0)))
    q_ext = q_ext.astype(bf16)
    k_ext = (k_ext * -BIG).astype(bf16)
    one_row = jnp.where(row == 0, 1.0, 0.0).astype(bf16)
    two_rows = jnp.where(row < 2, 1.0, 0.0).astype(bf16)

    bqT = jnp.transpose(jnp.broadcast_to(bq[...], (rows, bq.shape[1])))
    for win in range(windows):
        x = xs[win]
        mean = jnp.mean(x, axis=-1, keepdims=True)
        xc = x - mean
        var = jnp.mean(xc * xc, axis=-1, keepdims=True)
        normed = xc * lax.rsqrt(var + 1e-05) * gain[...] + nb[...]
        normT[win, :width, :] = jnp.transpose(normed).astype(bf16)
        normT[win, width:, :] = one_row
        attT[win, width:, :] = one_row
        qkvT[win] = (mm(wT[...], normT[win, :width, :]) + bqT).astype(bf16)
        gN[win] = gs[win].astype(bf16)
        doT[win] = mm(wp[...], gN[win], 1, 1).astype(bf16)

    def head(i, carry):
        win = i // HEADS
        h = i % HEADS
        at = pl.ds(pl.multiple_of(h * depth, depth), depth)
        at_k = pl.ds(pl.multiple_of(width + h * depth, depth), depth)
        at_v = pl.ds(pl.multiple_of(2 * width + h * depth, depth), depth)
        qT = qkvT[win, at, :]
        kT = qkvT[win, at_k, :]
        vT = qkvT[win, at_v, :]
        d_oT = doT[win, at, :]
        sT = mm(jnp.concatenate([kT, k_ext], 0), jnp.concatenate([qT, q_ext], 0), 0, 0)
        top = jnp.max(sT, axis=0, keepdims=True)
        e = jnp.exp2((sT - top) * (scale * math.log2(math.e)))
        eb = e.astype(bf16)
        summed = mm(jnp.concatenate([vT, one_row], 0), eb)
        inv = 1.0 / summed[depth : depth + 1]
        oT = (summed[:depth] * inv).astype(bf16)
        attT[win, at, :] = oT
        d_o = d_oT.astype(f32)
        delta = jnp.sum(d_o * oT.astype(f32), axis=0, keepdims=True) * inv
        d_on = (d_o * inv).astype(bf16)
        hi = delta.astype(bf16).astype(f32)
        lo = delta - hi
        d_ext = jnp.where(row == 0, -hi, jnp.where(row == 1, -lo, 0.0)).astype(bf16)
        dpT = mm(jnp.concatenate([vT, two_rows], 0), jnp.concatenate([d_on, d_ext], 0), 0, 0)
        dsT = (e * dpT).astype(bf16)
        dqT[win, at_v, :] = mm(d_on, eb, 1, 1).astype(bf16)
        dqT[win, at, :] = (mm(kT, dsT) * scale).astype(bf16)
        dqT[win, at_k, :] = (mm(qT, dsT, 1, 1) * scale).astype(bf16)
        return carry

    lax.fori_loop(0, windows * HEADS, head, 0)

    for win in range(windows):
        wide = 3 * width
        dw = mm(normT[win], dqT[win], 1, 1)
        dp = mm(attT[win], gN[win])
        if win == 0:
            acc[: width + EXT, :wide] = dw
            acc[: width + EXT, wide:] = dp
        else:
            acc[: width + EXT, :wide] += dw
            acc[: width + EXT, wide:] += dp
        gs[win] = jnp.transpose(mm(wpT[...], attT[win, :width, :])) + bp[...]
        for u in range(WT):
            b_u = (gs[win, pl.ds(u * patch, patch), :] * valid_of(u)).astype(bf16)
            if u < HALF:
                x_u = tok[HALF + u, win].astype(f32)
                mixed[HALF + u, win] = (x_u + b_u.astype(f32)).astype(bf16)
            else:
                send[0, u - HALF, win] = b_u
        dn = jnp.transpose(mm(w[...], dqT[win]).astype(bf16).astype(f32))
        x = xs[win]
        mean = jnp.mean(x, axis=-1, keepdims=True)
        xc = x - mean
        rstd = lax.rsqrt(jnp.mean(xc * xc, axis=-1, keepdims=True) + 1e-05)
        xhat = xc * rstd
        dgain = jnp.sum(dn * xhat, axis=0, keepdims=True)
        dbias = jnp.sum(dn, axis=0, keepdims=True)
        if win == 0:
            acc[width + EXT : width + EXT + 1, :width] = dgain
            acc[width + EXT : width + EXT + 1, width : 2 * width] = dbias
        else:
            acc[width + EXT : width + EXT + 1, :width] += dgain
            acc[width + EXT : width + EXT + 1, width : 2 * width] += dbias
        dxh = dn * gain[...]
        m1 = jnp.mean(dxh, axis=-1, keepdims=True)
        m2 = jnp.mean(dxh * xhat, axis=-1, keepdims=True)
        xs[win] = rstd * (dxh - m1 - xhat * m2)
        for u in range(WT):
            d_u = xs[win, pl.ds(u * patch, patch), :].astype(bf16)
            if u < HALF:
                g_u = gr[HALF + u, win].astype(f32)
                gtok[HALF + u, win] = (g_u + d_u.astype(f32)).astype(bf16)
            else:
                send[1, u - HALF, win] = d_u
    acc[width + EXT : width + EXT + 1, 2 * width :] = jnp.zeros((1, 2 * width), f32)
    acc[width + EXT + 1 :, :] = jnp.zeros((EXT - 1, 4 * width), f32)
    chunks, deep, lanes = pay.shape
    across = 4 * width // lanes
    for c in range(chunks):
        r, k = c // across, c % across
        pay[c] = acc[r * deep : (r + 1) * deep, k * lanes : (k + 1) * lanes].astype(bf16)


def final_kernel(
    width, recv, tok, gr, got, mixed_in, gtok_in,
    mixed, gtok, dgain, dnb, dwq, dbq, dwp, dbp, full,
):
    mixed[...] = (tok[...].astype(f32) + recv[0].astype(f32)).astype(bf16)
    gtok[...] = (gr[...].astype(f32) + recv[1].astype(f32)).astype(bf16)
    chunks, deep, lanes = got.shape
    across = 4 * width // lanes
    for c in range(chunks):
        r, k = c // across, c % across
        full[r * deep : (r + 1) * deep, k * lanes : (k + 1) * lanes] = got[c].astype(f32)
    dwq[...] = full[:width, : 3 * width]
    dwp[...] = full[:width, 3 * width :]
    dbq[...] = full[width : width + 1, : 3 * width]
    dbp[...] = full[width : width + 1, 3 * width :]
    dgain[...] = full[width + EXT : width + EXT + 1, :width]
    dnb[...] = full[width + EXT : width + EXT + 1, width : 2 * width]


def groups_of(bits, devices):
    offsets = []
    for m in range(1 << len(bits)):
        offsets.append(sum(1 << b for k, b in enumerate(bits) if m >> k & 1))
    mask = sum(1 << b for b in bits)
    return [[base | o for o in offsets] for base in range(devices) if not base & mask]


def exchange(x, bits):
    devices = lax.axis_size(AXES)
    return lax.all_to_all(
        x, AXES, 0, 0, tiled=True, axis_index_groups=groups_of(bits, devices)
    )


NEAR = (0, 1, 5, 6, 7)
ALONG_Z = (2, 3, 4)


def per_device(
    tokens, lengths, norm_gain, norm_bias, qkv_weight, qkv_bias, proj_weight, proj_bias, grad_out
):
    _, frames, windows, patch, width = tokens.shape
    rows = WT * patch
    frame_total = frames * lax.axis_size("frame")
    first = lax.axis_index("frame") * frames + HALF
    tok, gr = tokens[0], grad_out[0]
    halo = passed_along(jnp.stack([tok[:HALF], gr[:HALF]]), "frame", -1)
    w = qkv_weight.astype(bf16)
    wp = proj_weight.astype(bf16)
    sc = jnp.stack([lengths[0], first]).astype(jnp.int32)
    vmem = pl.BlockSpec(memory_space=pltpu.VMEM)
    near = 1 << len(NEAR)
    deep = (width + 2 * EXT) * 4 * width // 128 // near
    half = (HALF, windows, patch, width)
    slab = jax.ShapeDtypeStruct(tok.shape, bf16)
    mixed, gtok, send, pay = pl.pallas_call(
        functools.partial(block_kernel, frame_total),
        name="block",
        out_shape=(
            slab,
            slab,
            jax.ShapeDtypeStruct((2,) + half, bf16),
            jax.ShapeDtypeStruct((near, deep, 128), bf16),
        ),
        in_specs=[pl.BlockSpec(memory_space=pltpu.SMEM)] + [vmem] * 11,
        out_specs=(vmem,) * 4,
        scratch_shapes=[
            pltpu.VMEM((windows, rows, width), f32),
            pltpu.VMEM((windows, rows, width), f32),
            pltpu.VMEM((windows, width + EXT, rows), bf16),
            pltpu.VMEM((windows, rows, width), bf16),
            pltpu.VMEM((windows, 3 * width, rows), bf16),
            pltpu.VMEM((windows, width, rows), bf16),
            pltpu.VMEM((windows, width + EXT, rows), bf16),
            pltpu.VMEM((windows, 3 * width, rows), bf16),
            pltpu.VMEM((width + 2 * EXT, 4 * width), f32),
        ],
        compiler_params=pltpu.CompilerParams(vmem_limit_bytes=48 << 20),
    )(
        sc, tok, gr, halo, norm_gain[None], norm_bias[None], w, w.T, wp, wp.T,
        qkv_bias[None], proj_bias[None],
    )
    recv = passed_along(send, "frame", 1)
    part = jnp.sum(exchange(pay, NEAR).astype(f32), axis=0)
    deeper = 1 << len(ALONG_Z)
    total = jnp.sum(exchange(jnp.broadcast_to(part, (deeper,) + part.shape), ALONG_Z), axis=0)
    got = exchange(jnp.broadcast_to(total.astype(bf16), (near,) + part.shape), NEAR)

    def whole(*shape):
        return pl.BlockSpec(shape, lambda i: (0,) * len(shape))

    anywhere = pl.BlockSpec(memory_space=pl.ANY)
    mixed, gtok, dgain, dnb, dwq, dbq, dwp, dbp = pl.pallas_call(
        functools.partial(final_kernel, width),
        name="final",
        grid=(1,),
        out_shape=(
            slab,
            slab,
            jax.ShapeDtypeStruct((1, width), f32),
            jax.ShapeDtypeStruct((1, width), f32),
            jax.ShapeDtypeStruct((width, 3 * width), f32),
            jax.ShapeDtypeStruct((1, 3 * width), f32),
            jax.ShapeDtypeStruct((width, width), f32),
            jax.ShapeDtypeStruct((1, width), f32),
        ),
        in_specs=[
            whole(2, *half), whole(*half), whole(*half), whole(near, deep, 128),
            anywhere, anywhere,
        ],
        out_specs=(
            whole(*half), whole(*half), whole(1, width), whole(1, width),
            whole(width, 3 * width), whole(1, 3 * width), whole(width, width), whole(1, width),
        ),
        scratch_shapes=[pltpu.VMEM((width + 2 * EXT, 4 * width), f32)],
        input_output_aliases={4: 0, 5: 1},
        compiler_params=pltpu.CompilerParams(vmem_limit_bytes=32 << 20),
    )(recv, tok, gr, got, mixed, gtok)
    return (mixed[None], gtok[None], dgain[0], dnb[0], dwq, dbq[0], dwp, dbp[0])


def solution(mesh):
    split = P("clip", "frame", None, None, None)
    in_specs = (split, P("clip"), P(), P(), P(), P(), P(), P(), split)
    out_specs = (split, split, P(), P(), P(), P(), P(), P())
    return jax.shard_map(
        per_device, mesh=mesh, in_specs=in_specs, out_specs=out_specs, check_vma=False
    )
```

```python
import functools
import math

import jax
import jax.numpy as jnp
from jax import lax
from jax.experimental import pallas as pl
from jax.experimental.pallas import tpu as pltpu
from jax.sharding import PartitionSpec as P

HEADS = 8
WT = 8
HALF = WT // 2
AXES = ("frame", "clip")
BIG = 2.0**100
UNROLL = 2
EXT = 16
f32, bf16 = jnp.float32, jnp.bfloat16


def swapped(array, odd):
    devices = lax.axis_size("frame")
    pairs = [(i, (((i + odd) ^ 1) - odd) % devices) for i in range(devices)]
    return lax.ppermute(array, "frame", pairs)


def mm(a, b, ca=1, cb=0):
    return lax.dot_general(a, b, (((ca,), (cb,)), ((), ())), preferred_element_type=f32)


def role(place, odd, frames):
    first = lax.rem(place, 2) == odd
    own_start = jnp.where(first, HALF, 0)
    win = jnp.where(first, 0, 1)
    return first, own_start, win


def pick_kernel(tok, gr, out):
    _, start, win = role(lax.axis_index("frame"), 1, tok.shape[0])
    for k in range(HALF):
        out[0, k] = tok[start + k, 1 - win]
        out[1, k] = gr[start + k, 1 - win]


def block_kernel(
    frame_total, last, lengths, tok, gr, halo, gain, nb, w, wT, wp, wpT, bq, bp, *refs
):
    if last:
        acc_in, mixed, gtok, send, pay = refs[:5]
    else:
        mixed, gtok, send, acc_out = refs[:4]
    xs, gs, normT, gN, qkvT, doT, attT, dqT, acc, ext = refs[-10:]
    patch, width = tok.shape[2:]
    rows = WT * patch
    depth = width // HEADS
    scale = depth ** (-0.5)
    length = lengths[0]
    frames = tok.shape[0]
    place = lax.axis_index("frame")
    first, own_start, win = role(place, int(last), frames)
    own_frame = place * frames + own_start
    halo_frame = place * frames + jnp.where(first, frames, -HALF)
    halo_frame = jnp.where(halo_frame < 0, halo_frame + frame_total, halo_frame)
    halo_frame = jnp.where(halo_frame >= frame_total, halo_frame - frame_total, halo_frame)

    def valid_of(u):
        t = own_frame + u if u < HALF else halo_frame + (u - HALF)
        return jnp.where(t < length, 1.0, 0.0).astype(f32)

    for u in range(WT):
        at = pl.ds(u * patch, patch)
        k = u % HALF
        if u < HALF:
            x_u, g_u = tok[own_start + k, win], gr[own_start + k, win]
        else:
            x_u, g_u = halo[0, k], halo[1, k]
        xs[at, :] = x_u.astype(f32)
        gs[at, :] = g_u.astype(f32) * valid_of(u)

    lane = lax.broadcasted_iota(jnp.int32, (EXT, rows), 1)
    row = lax.broadcasted_iota(jnp.int32, (EXT, rows), 0)
    u_lane = jnp.zeros((EXT, rows), jnp.int32)
    for u in range(1, WT):
        u_lane = u_lane + jnp.where(lane >= u * patch, 1, 0)
    t_lane = jnp.where(u_lane < HALF, own_frame + u_lane, halo_frame + u_lane - HALF)
    bad = jnp.where(t_lane < length, 0.0, 1.0)
    reg = jnp.where(t_lane < HALF, 1.0, 0.0)
    q_rows = jnp.where(row == 1, reg, jnp.where(row == 2, 1.0 - reg, 0.0))
    k_rows = jnp.where(row == 1, 1.0 - reg, jnp.where(row == 2, reg, 0.0))
    ext[0] = jnp.where(row == 0, 1.0, q_rows).astype(bf16)
    ext[1] = (jnp.where(row == 0, bad, k_rows) * -BIG).astype(bf16)
    one_row = jnp.where(row == 0, 1.0, 0.0).astype(bf16)
    two_rows = jnp.where(row < 2, 1.0, 0.0).astype(bf16)

    bqT = jnp.transpose(jnp.broadcast_to(bq[...], (rows, bq.shape[1])))
    x = xs[...]
    mean = jnp.mean(x, axis=-1, keepdims=True)
    xc = x - mean
    var = jnp.mean(xc * xc, axis=-1, keepdims=True)
    rstd = lax.rsqrt(var + 1e-05)
    xhat = xc * rstd
    xs[...] = xhat
    normed = xhat * gain[...] + nb[...]
    normT[:width, :] = jnp.transpose(normed).astype(bf16)
    normT[width:, :] = one_row
    attT[width:, :] = one_row
    qkvT[...] = (mm(wT[...], normT[:width, :]) + bqT).astype(bf16)
    gN[...] = gs[...].astype(bf16)
    doT[...] = mm(wp[...], gN[...], 1, 1).astype(bf16)

    def head(h):
        at = pl.ds(pl.multiple_of(h * depth, depth), depth)
        at_k = pl.ds(pl.multiple_of(width + h * depth, depth), depth)
        at_v = pl.ds(pl.multiple_of(2 * width + h * depth, depth), depth)
        qT = qkvT[at, :]
        kT = qkvT[at_k, :]
        vT = qkvT[at_v, :]
        d_oT = doT[at, :]
        sT = mm(jnp.concatenate([kT, ext[1]], 0), jnp.concatenate([qT, ext[0]], 0), 0, 0)
        top = jnp.max(sT, axis=0, keepdims=True)
        e = jnp.exp2((sT - top) * (scale * math.log2(math.e)))
        eb = e.astype(bf16)
        summed = mm(jnp.concatenate([vT, one_row], 0), eb)
        inv = 1.0 / summed[depth : depth + 1]
        oT = (summed[:depth] * inv).astype(bf16)
        attT[at, :] = oT
        d_o = d_oT.astype(f32)
        delta = jnp.sum(d_o * oT.astype(f32), axis=0, keepdims=True) * inv
        d_on = (d_o * inv).astype(bf16)
        hi = delta.astype(bf16).astype(f32)
        lo = delta - hi
        d_ext = jnp.where(row == 0, -hi, jnp.where(row == 1, -lo, 0.0)).astype(bf16)
        dpT = mm(jnp.concatenate([vT, two_rows], 0), jnp.concatenate([d_on, d_ext], 0), 0, 0)
        dsT = (e * dpT).astype(bf16)
        dqT[at_v, :] = mm(d_on, eb, 1, 1).astype(bf16)
        dqT[at, :] = (mm(kT, dsT) * scale).astype(bf16)
        dqT[at_k, :] = (mm(qT, dsT, 1, 1) * scale).astype(bf16)

    def heads(i, carry):
        for k in range(UNROLL):
            head(i * UNROLL + k)
        return carry

    lax.fori_loop(0, HEADS // UNROLL, heads, 0)

    wide = 3 * width
    acc[: width + EXT, :wide] = mm(normT[...], dqT[...], 1, 1)
    acc[: width + EXT, wide:] = mm(attT[...], gN[...])
    gs[...] = jnp.transpose(mm(wpT[...], attT[:width, :])) + bp[...]
    for u in range(WT):
        k = u % HALF
        b_u = (gs[pl.ds(u * patch, patch), :] * valid_of(u)).astype(bf16)
        if u < HALF:
            x_u = tok[own_start + k, win].astype(f32)
            mixed[k] = (x_u + b_u.astype(f32)).astype(bf16)
        else:
            send[0, k] = b_u
    dn = jnp.transpose(mm(w[...], dqT[...]).astype(bf16).astype(f32))
    xhat = xs[...]
    small = width + EXT
    acc[small : small + 1, :width] = jnp.sum(dn * xhat, axis=0, keepdims=True)
    acc[small : small + 1, width : 2 * width] = jnp.sum(dn, axis=0, keepdims=True)
    acc[small : small + 1, 2 * width :] = jnp.zeros((1, 2 * width), f32)
    acc[small + 1 :, :] = jnp.zeros((EXT - 1, 4 * width), f32)
    dxh = dn * gain[...]
    m1 = jnp.mean(dxh, axis=-1, keepdims=True)
    m2 = jnp.mean(dxh * xhat, axis=-1, keepdims=True)
    gs[...] = rstd * (dxh - m1 - xhat * m2)
    for u in range(WT):
        k = u % HALF
        d_u = gs[pl.ds(u * patch, patch), :].astype(bf16)
        if u < HALF:
            g_u = gr[own_start + k, win].astype(f32)
            gtok[k] = (g_u + d_u.astype(f32)).astype(bf16)
        else:
            send[1, k] = d_u
    if not last:
        acc_out[...] = acc[...]
    else:
        chunks, deep, lanes = pay.shape
        across = 4 * width // lanes
        for c in range(chunks):
            r, k = c // across, c % across
            at = (slice(r * deep, (r + 1) * deep), slice(k * lanes, (k + 1) * lanes))
            pay[c] = (acc_in[at] + acc[at]).astype(bf16)


def join_kernel(tok, gr, mixed1, gtok1, back1, mixed2, gtok2, back2, mixed, gtok):
    for n, (m, g, back) in enumerate(((mixed1, gtok1, back1), (mixed2, gtok2, back2))):
        _, start, win = role(lax.axis_index("frame"), n, tok.shape[0])
        other, other_win = start, 1 - win
        for k in range(HALF):
            mixed[start + k, win] = m[k]
            gtok[start + k, win] = g[k]
            at = other + k
            mixed[at, other_win] = (
                tok[at, other_win].astype(f32) + back[0, k].astype(f32)
            ).astype(bf16)
            gtok[at, other_win] = (
                gr[at, other_win].astype(f32) + back[1, k].astype(f32)
            ).astype(bf16)


def unpack_kernel(width, got, dgain, dnb, dwq, dbq, dwp, dbp, full):
    chunks, deep, lanes = got.shape
    across = 4 * width // lanes
    for c in range(chunks):
        r, k = c // across, c % across
        full[r * deep : (r + 1) * deep, k * lanes : (k + 1) * lanes] = got[c].astype(f32)
    dwq[...] = full[:width, : 3 * width]
    dwp[...] = full[:width, 3 * width :]
    dbq[...] = full[width : width + 1, : 3 * width]
    dbp[...] = full[width : width + 1, 3 * width :]
    dgain[...] = full[width + EXT : width + EXT + 1, :width]
    dnb[...] = full[width + EXT : width + EXT + 1, width : 2 * width]


def groups_of(bits, devices):
    offsets = []
    for m in range(1 << len(bits)):
        offsets.append(sum(1 << b for k, b in enumerate(bits) if m >> k & 1))
    mask = sum(1 << b for b in bits)
    return [[base | o for o in offsets] for base in range(devices) if not base & mask]


def exchange(x, bits):
    devices = lax.axis_size(AXES)
    return lax.all_to_all(
        x, AXES, 0, 0, tiled=True, axis_index_groups=groups_of(bits, devices)
    )


NEAR = (0, 1, 5, 6, 7)
ALONG_Z = (2, 3, 4)


def per_device(
    tokens, lengths, norm_gain, norm_bias, qkv_weight, qkv_bias, proj_weight, proj_bias, grad_out
):
    _, frames, windows, patch, width = tokens.shape
    rows = WT * patch
    frame_total = frames * lax.axis_size("frame")
    place = lax.axis_index("frame")
    tok, gr = tokens[0], grad_out[0]
    vmem = pl.BlockSpec(memory_space=pltpu.VMEM)
    smem = pl.BlockSpec(memory_space=pltpu.SMEM)
    half = jax.ShapeDtypeStruct((HALF, patch, width), bf16)
    halves = jax.ShapeDtypeStruct((2, HALF, patch, width), bf16)

    _, own_start, win = role(place, 0, frames)
    size = (1, HALF, 1, patch, width)
    at = (0, own_start, 1 - win, 0, 0)
    give1 = jnp.concatenate(
        [lax.dynamic_slice(a, at, size)[0, :, 0][None] for a in (tokens, grad_out)]
    )
    halo1 = swapped(give1, 0)
    give2 = pl.pallas_call(
        pick_kernel,
        name="pick",
        out_shape=halves,
        in_specs=[vmem] * 2,
        out_specs=vmem,
        compiler_params=pltpu.CompilerParams(vmem_limit_bytes=8 << 20),
    )(tok, gr)
    halo2 = swapped(give2, 1)
    w = qkv_weight.astype(bf16)
    wp = proj_weight.astype(bf16)
    near = 1 << len(NEAR)
    deep = (width + 2 * EXT) * 4 * width // 128 // near
    total_rows = width + 2 * EXT
    sums_type = jax.ShapeDtypeStruct((total_rows, 4 * width), f32)
    pay_type = jax.ShapeDtypeStruct((near, deep, 128), bf16)

    def block(last, halo, *more):
        return pl.pallas_call(
            functools.partial(block_kernel, frame_total, last),
            name="second_window" if last else "first_window",
            out_shape=(half, half, halves, pay_type if last else sums_type),
            in_specs=[smem] + [vmem] * (11 + len(more)),
            out_specs=(vmem,) * 4,
            scratch_shapes=[
                pltpu.VMEM((rows, width), f32),
                pltpu.VMEM((rows, width), f32),
                pltpu.VMEM((width + EXT, rows), bf16),
                pltpu.VMEM((rows, width), bf16),
                pltpu.VMEM((3 * width, rows), bf16),
                pltpu.VMEM((width, rows), bf16),
                pltpu.VMEM((width + EXT, rows), bf16),
                pltpu.VMEM((3 * width, rows), bf16),
                pltpu.VMEM((total_rows, 4 * width), f32),
                pltpu.VMEM((2, EXT, rows), bf16),
            ],
            compiler_params=pltpu.CompilerParams(vmem_limit_bytes=32 << 20),
            cost_estimate=pl.CostEstimate(
                flops=8_000_000_000, bytes_accessed=8_000_000, transcendentals=2_000_000
            ),
        )(
            lengths, tok, gr, halo, norm_gain[None], norm_bias[None], w, w.T, wp, wp.T,
            qkv_bias[None], proj_bias[None], *more,
        )

    mixed1, gtok1, send1, sums1 = block(False, halo1)
    back1 = swapped(send1, 0)
    mixed2, gtok2, send2, pay = block(True, halo2, sums1)
    pay, back1 = lax.optimization_barrier((pay, back1))
    part = jnp.sum(exchange(pay, NEAR).astype(f32), axis=0).astype(bf16)
    deeper = 1 << len(ALONG_Z)
    sums = exchange(jnp.broadcast_to(part, (deeper,) + part.shape), ALONG_Z)
    total = jnp.sum(sums.astype(f32), axis=0).astype(bf16)
    back2 = swapped(send2, 1)
    got = exchange(jnp.broadcast_to(total, (near,) + part.shape), NEAR)
    slab = jax.ShapeDtypeStruct(tok.shape, bf16)
    mixed, gtok = pl.pallas_call(
        join_kernel,
        name="join",
        out_shape=(slab, slab),
        in_specs=[vmem] * 8,
        out_specs=(vmem,) * 2,
        compiler_params=pltpu.CompilerParams(vmem_limit_bytes=16 << 20),
        cost_estimate=pl.CostEstimate(
            flops=20_000_000_000, bytes_accessed=4_000_000, transcendentals=0
        ),
    )(
        tok, gr,
        mixed1, gtok1, back1, mixed2, gtok2, back2,
    )
    dgain, dnb, dwq, dbq, dwp, dbp = pl.pallas_call(
        functools.partial(unpack_kernel, width),
        name="unpack",
        out_shape=(
            jax.ShapeDtypeStruct((1, width), f32),
            jax.ShapeDtypeStruct((1, width), f32),
            jax.ShapeDtypeStruct((width, 3 * width), f32),
            jax.ShapeDtypeStruct((1, 3 * width), f32),
            jax.ShapeDtypeStruct((width, width), f32),
            jax.ShapeDtypeStruct((1, width), f32),
        ),
        in_specs=[vmem],
        out_specs=(vmem,) * 6,
        scratch_shapes=[pltpu.VMEM((width + 2 * EXT, 4 * width), f32)],
        compiler_params=pltpu.CompilerParams(vmem_limit_bytes=16 << 20),
    )(got)
    return (mixed[None], gtok[None], dgain[0], dnb[0], dwq, dbq[0], dwp, dbp[0])


def solution(mesh):
    split = P("clip", "frame", None, None, None)
    in_specs = (split, P("clip"), P(), P(), P(), P(), P(), P(), split)
    out_specs = (split, split, P(), P(), P(), P(), P(), P())
    return jax.shard_map(
        per_device, mesh=mesh, in_specs=in_specs, out_specs=out_specs, check_vma=False
    )
```

```python
import functools
import math

import jax
import jax.numpy as jnp
from jax import lax
from jax.experimental import pallas as pl
from jax.experimental.pallas import tpu as pltpu
from jax.sharding import PartitionSpec as P

HEADS = 8
WT = 8
HALF = WT // 2
AXES = ("frame", "clip")
BIG = 2.0**100
UNROLL = 8
EXT = 16
f32, bf16 = jnp.float32, jnp.bfloat16


def swapped(array, odd):
    devices = lax.axis_size("frame")
    pairs = [(i, (((i + odd) ^ 1) - odd) % devices) for i in range(devices)]
    return lax.ppermute(array, "frame", pairs)


def mm(a, b, ca=1, cb=0):
    return lax.dot_general(a, b, (((ca,), (cb,)), ((), ())), preferred_element_type=f32)


def role(place, odd, frames):
    first = lax.rem(place, 2) == odd
    own_start = jnp.where(first, HALF, 0)
    win = jnp.where(first, 0, 1)
    return first, own_start, win


def pick_kernel(tok, gr, out):
    _, start, win = role(lax.axis_index("frame"), 1, tok.shape[0])
    for k in range(HALF):
        out[0, k] = tok[start + k, 1 - win]
        out[1, k] = gr[start + k, 1 - win]


def block_kernel(
    frame_total, last, lengths, tok, gr, halo, gain, nb, w32, wp32, bq, bp, *refs
):
    if last:
        acc_in, mixed, gtok, send, pay = refs[:5]
    else:
        mixed, gtok, send, acc_out = refs[:4]
    xs, gs, normT, gN, qkvT, doT, attT, dqT, acc, ext, w, wp = refs[-12:]
    w[...] = w32[...].astype(bf16)
    wp[...] = wp32[...].astype(bf16)
    patch, width = tok.shape[2:]
    rows = WT * patch
    depth = width // HEADS
    scale = depth ** (-0.5)
    length = lengths[0]
    frames = tok.shape[0]
    place = lax.axis_index("frame")
    first, own_start, win = role(place, int(last), frames)
    own_frame = place * frames + own_start
    halo_frame = place * frames + jnp.where(first, frames, -HALF)
    halo_frame = jnp.where(halo_frame < 0, halo_frame + frame_total, halo_frame)
    halo_frame = jnp.where(halo_frame >= frame_total, halo_frame - frame_total, halo_frame)

    def valid_of(u):
        t = own_frame + u if u < HALF else halo_frame + (u - HALF)
        return jnp.where(t < length, 1.0, 0.0).astype(f32)

    for u in range(WT):
        at = pl.ds(u * patch, patch)
        k = u % HALF
        if u < HALF:
            x_u, g_u = tok[own_start + k, win], gr[own_start + k, win]
        else:
            x_u, g_u = halo[0, k], halo[1, k]
        xs[at, :] = x_u.astype(f32)
        gs[at, :] = g_u.astype(f32) * valid_of(u)

    lane = lax.broadcasted_iota(jnp.int32, (EXT, rows), 1)
    row = lax.broadcasted_iota(jnp.int32, (EXT, rows), 0)
    u_lane = jnp.zeros((EXT, rows), jnp.int32)
    for u in range(1, WT):
        u_lane = u_lane + jnp.where(lane >= u * patch, 1, 0)
    t_lane = jnp.where(u_lane < HALF, own_frame + u_lane, halo_frame + u_lane - HALF)
    bad = jnp.where(t_lane < length, 0.0, 1.0)
    reg = jnp.where(t_lane < HALF, 1.0, 0.0)
    q_rows = jnp.where(row == 1, reg, jnp.where(row == 2, 1.0 - reg, 0.0))
    k_rows = jnp.where(row == 1, 1.0 - reg, jnp.where(row == 2, reg, 0.0))
    ext[0] = jnp.where(row == 0, 1.0, q_rows).astype(bf16)
    ext[1] = (jnp.where(row == 0, bad, k_rows) * -BIG).astype(bf16)
    one_row = jnp.where(row == 0, 1.0, 0.0).astype(bf16)
    two_rows = jnp.where(row < 2, 1.0, 0.0).astype(bf16)

    bqT = jnp.transpose(jnp.broadcast_to(bq[...], (rows, bq.shape[1])))
    x = xs[...]
    mean = jnp.mean(x, axis=-1, keepdims=True)
    xc = x - mean
    var = jnp.mean(xc * xc, axis=-1, keepdims=True)
    rstd = lax.rsqrt(var + 1e-05)
    xhat = xc * rstd
    xs[...] = xhat
    normed = xhat * gain[...] + nb[...]
    normT[:width, :] = jnp.transpose(normed).astype(bf16)
    normT[width:, :] = one_row
    attT[width:, :] = one_row
    qkvT[...] = (mm(w[...], normT[:width, :], 0, 0) + bqT).astype(bf16)
    gN[...] = gs[...].astype(bf16)
    doT[...] = mm(wp[...], gN[...], 1, 1).astype(bf16)

    def head(h):
        at = pl.ds(pl.multiple_of(h * depth, depth), depth)
        at_k = pl.ds(pl.multiple_of(width + h * depth, depth), depth)
        at_v = pl.ds(pl.multiple_of(2 * width + h * depth, depth), depth)
        qT = qkvT[at, :]
        kT = qkvT[at_k, :]
        vT = qkvT[at_v, :]
        d_oT = doT[at, :]
        sT = mm(jnp.concatenate([kT, ext[1]], 0), jnp.concatenate([qT, ext[0]], 0), 0, 0)
        top = jnp.max(sT, axis=0, keepdims=True)
        e = jnp.exp2((sT - top) * (scale * math.log2(math.e)))
        eb = e.astype(bf16)
        summed = mm(jnp.concatenate([vT, one_row], 0), eb)
        inv = 1.0 / summed[depth : depth + 1]
        oT = (summed[:depth] * inv).astype(bf16)
        attT[at, :] = oT
        d_o = d_oT.astype(f32)
        delta = jnp.sum(d_o * oT.astype(f32), axis=0, keepdims=True) * inv
        d_on = (d_o * inv).astype(bf16)
        hi = delta.astype(bf16).astype(f32)
        lo = delta - hi
        d_ext = jnp.where(row == 0, -hi, jnp.where(row == 1, -lo, 0.0)).astype(bf16)
        dpT = mm(jnp.concatenate([vT, two_rows], 0), jnp.concatenate([d_on, d_ext], 0), 0, 0)
        dsT = (e * dpT).astype(bf16)
        dqT[at_v, :] = mm(d_on, eb, 1, 1).astype(bf16)
        dqT[at, :] = (mm(kT, dsT) * scale).astype(bf16)
        dqT[at_k, :] = (mm(qT, dsT, 1, 1) * scale).astype(bf16)

    def heads(i, carry):
        for k in range(UNROLL):
            head(i * UNROLL + k)
        return carry

    lax.fori_loop(0, HEADS // UNROLL, heads, 0)

    wide = 3 * width
    acc[: width + EXT, :wide] = mm(normT[...], dqT[...], 1, 1)
    acc[: width + EXT, wide:] = mm(attT[...], gN[...])
    gs[...] = jnp.transpose(mm(wp[...], attT[:width, :], 0, 0)) + bp[...]
    for u in range(WT):
        k = u % HALF
        b_u = (gs[pl.ds(u * patch, patch), :] * valid_of(u)).astype(bf16)
        if u < HALF:
            x_u = tok[own_start + k, win].astype(f32)
            mixed[k] = (x_u + b_u.astype(f32)).astype(bf16)
        else:
            send[0, k] = b_u
    dn = jnp.transpose(mm(w[...], dqT[...]).astype(bf16).astype(f32))
    xhat = xs[...]
    small = width + EXT
    acc[small : small + 1, :width] = jnp.sum(dn * xhat, axis=0, keepdims=True)
    acc[small : small + 1, width : 2 * width] = jnp.sum(dn, axis=0, keepdims=True)
    acc[small : small + 1, 2 * width :] = jnp.zeros((1, 2 * width), f32)
    acc[small + 1 :, :] = jnp.zeros((EXT - 1, 4 * width), f32)
    dxh = dn * gain[...]
    m1 = jnp.mean(dxh, axis=-1, keepdims=True)
    m2 = jnp.mean(dxh * xhat, axis=-1, keepdims=True)
    gs[...] = rstd * (dxh - m1 - xhat * m2)
    for u in range(WT):
        k = u % HALF
        d_u = gs[pl.ds(u * patch, patch), :].astype(bf16)
        if u < HALF:
            g_u = gr[own_start + k, win].astype(f32)
            gtok[k] = (g_u + d_u.astype(f32)).astype(bf16)
        else:
            send[1, k] = d_u
    if not last:
        acc_out[...] = acc[...]
    else:
        chunks, deep, lanes = pay.shape
        across = 4 * width // lanes
        for c in range(chunks):
            r, k = c // across, c % across
            at = (slice(r * deep, (r + 1) * deep), slice(k * lanes, (k + 1) * lanes))
            pay[c] = (acc_in[at] + acc[at]).astype(bf16)


def join_kernel(tok, gr, mixed1, gtok1, back1, mixed2, gtok2, back2, mixed, gtok):
    for n, (m, g, back) in enumerate(((mixed1, gtok1, back1), (mixed2, gtok2, back2))):
        _, start, win = role(lax.axis_index("frame"), n, tok.shape[0])
        other, other_win = start, 1 - win
        for k in range(HALF):
            mixed[start + k, win] = m[k]
            gtok[start + k, win] = g[k]
            at = other + k
            mixed[at, other_win] = (
                tok[at, other_win].astype(f32) + back[0, k].astype(f32)
            ).astype(bf16)
            gtok[at, other_win] = (
                gr[at, other_win].astype(f32) + back[1, k].astype(f32)
            ).astype(bf16)


def spread_kernel(parts, out):
    total = parts[0].astype(f32)
    for k in range(1, parts.shape[0]):
        total = total + parts[k].astype(f32)
    total = total.astype(bf16)
    for k in range(out.shape[0]):
        out[k] = total


def spread(parts, copies):
    vmem = pl.BlockSpec(memory_space=pltpu.VMEM)
    return pl.pallas_call(
        spread_kernel,
        name="spread",
        out_shape=jax.ShapeDtypeStruct((copies,) + parts.shape[1:], bf16),
        in_specs=[vmem],
        out_specs=vmem,
        compiler_params=pltpu.CompilerParams(vmem_limit_bytes=8 << 20),
    )(parts)


def unpack_kernel(width, got, dgain, dnb, dwq, dbq, dwp, dbp, full):
    chunks, deep, lanes = got.shape
    across = 4 * width // lanes
    for c in range(chunks):
        r, k = c // across, c % across
        full[r * deep : (r + 1) * deep, k * lanes : (k + 1) * lanes] = got[c].astype(f32)
    dwq[...] = full[:width, : 3 * width]
    dwp[...] = full[:width, 3 * width :]
    dbq[...] = full[width, : 3 * width]
    dbp[...] = full[width, 3 * width :]
    dgain[...] = full[width + EXT, :width]
    dnb[...] = full[width + EXT, width : 2 * width]


def groups_of(bits, devices):
    offsets = []
    for m in range(1 << len(bits)):
        offsets.append(sum(1 << b for k, b in enumerate(bits) if m >> k & 1))
    mask = sum(1 << b for b in bits)
    return [[base | o for o in offsets] for base in range(devices) if not base & mask]


def exchange(x, bits):
    devices = lax.axis_size(AXES)
    return lax.all_to_all(
        x, AXES, 0, 0, tiled=True, axis_index_groups=groups_of(bits, devices)
    )


NEAR = (0, 1, 5, 6, 7)
ALONG_Z = (2, 3, 4)


def per_device(
    tokens, lengths, norm_gain, norm_bias, qkv_weight, qkv_bias, proj_weight, proj_bias, grad_out
):
    _, frames, windows, patch, width = tokens.shape
    rows = WT * patch
    frame_total = frames * lax.axis_size("frame")
    place = lax.axis_index("frame")
    tok, gr = tokens[0], grad_out[0]
    vmem = pl.BlockSpec(memory_space=pltpu.VMEM)
    smem = pl.BlockSpec(memory_space=pltpu.SMEM)
    half = jax.ShapeDtypeStruct((HALF, patch, width), bf16)
    halves = jax.ShapeDtypeStruct((2, HALF, patch, width), bf16)

    _, own_start, win = role(place, 0, frames)
    size = (1, HALF, 1, patch, width)
    at = (0, own_start, 1 - win, 0, 0)
    give1 = jnp.concatenate(
        [lax.dynamic_slice(a, at, size)[0, :, 0][None] for a in (tokens, grad_out)]
    )
    halo1 = swapped(give1, 0)
    give2 = pl.pallas_call(
        pick_kernel,
        name="pick",
        out_shape=halves,
        in_specs=[vmem] * 2,
        out_specs=vmem,
        compiler_params=pltpu.CompilerParams(vmem_limit_bytes=8 << 20),
    )(tok, gr)
    halo2 = swapped(give2, 1)
    near = 1 << len(NEAR)
    deep = (width + 2 * EXT) * 4 * width // 128 // near
    total_rows = width + 2 * EXT
    sums_type = jax.ShapeDtypeStruct((total_rows, 4 * width), f32)
    pay_type = jax.ShapeDtypeStruct((near, deep, 128), bf16)

    def block(last, halo, *more):
        return pl.pallas_call(
            functools.partial(block_kernel, frame_total, last),
            name="second_window" if last else "first_window",
            out_shape=(half, half, halves, pay_type if last else sums_type),
            in_specs=[smem] + [vmem] * (9 + len(more)),
            out_specs=(vmem,) * 4,
            scratch_shapes=[
                pltpu.VMEM((rows, width), f32),
                pltpu.VMEM((rows, width), f32),
                pltpu.VMEM((width + EXT, rows), bf16),
                pltpu.VMEM((rows, width), bf16),
                pltpu.VMEM((3 * width, rows), bf16),
                pltpu.VMEM((width, rows), bf16),
                pltpu.VMEM((width + EXT, rows), bf16),
                pltpu.VMEM((3 * width, rows), bf16),
                pltpu.VMEM((total_rows, 4 * width), f32),
                pltpu.VMEM((2, EXT, rows), bf16),
                pltpu.VMEM((width, 3 * width), bf16),
                pltpu.VMEM((width, width), bf16),
            ],
            compiler_params=pltpu.CompilerParams(vmem_limit_bytes=32 << 20),
            cost_estimate=pl.CostEstimate(
                flops=8_000_000_000, bytes_accessed=8_000_000, transcendentals=2_000_000
            ),
        )(
            lengths, tok, gr, halo, norm_gain[None], norm_bias[None], qkv_weight,
            proj_weight, qkv_bias[None], proj_bias[None], *more,
        )

    mixed1, gtok1, send1, sums1 = block(False, halo1)
    back1 = swapped(send1, 0)
    mixed2, gtok2, send2, pay = block(True, halo2, sums1)
    pay, back1 = lax.optimization_barrier((pay, back1))
    back2 = swapped(send2, 1)
    part = spread(exchange(pay, NEAR), 1 << len(ALONG_Z))
    total = spread(exchange(part, ALONG_Z), near)
    got = exchange(total, NEAR)
    slab = jax.ShapeDtypeStruct(tok.shape, bf16)
    mixed, gtok = pl.pallas_call(
        join_kernel,
        name="join",
        out_shape=(slab, slab),
        in_specs=[vmem] * 8,
        out_specs=(vmem,) * 2,
        compiler_params=pltpu.CompilerParams(vmem_limit_bytes=16 << 20),
        cost_estimate=pl.CostEstimate(
            flops=20_000_000_000, bytes_accessed=4_000_000, transcendentals=0
        ),
    )(
        tok, gr,
        mixed1, gtok1, back1, mixed2, gtok2, back2,
    )
    dgain, dnb, dwq, dbq, dwp, dbp = pl.pallas_call(
        functools.partial(unpack_kernel, width),
        name="unpack",
        out_shape=(
            jax.ShapeDtypeStruct((width,), f32),
            jax.ShapeDtypeStruct((width,), f32),
            jax.ShapeDtypeStruct((width, 3 * width), f32),
            jax.ShapeDtypeStruct((3 * width,), f32),
            jax.ShapeDtypeStruct((width, width), f32),
            jax.ShapeDtypeStruct((width,), f32),
        ),
        in_specs=[vmem],
        out_specs=(vmem,) * 6,
        scratch_shapes=[pltpu.VMEM((width + 2 * EXT, 4 * width), f32)],
        compiler_params=pltpu.CompilerParams(vmem_limit_bytes=16 << 20),
    )(got)
    return (mixed[None], gtok[None], dgain, dnb, dwq, dbq, dwp, dbp)


def solution(mesh):
    split = P("clip", "frame", None, None, None)
    in_specs = (split, P("clip"), P(), P(), P(), P(), P(), P(), split)
    out_specs = (split, split, P(), P(), P(), P(), P(), P())
    return jax.shard_map(
        per_device, mesh=mesh, in_specs=in_specs, out_specs=out_specs, check_vma=False
    )
```

```python
import functools
import math

import jax
import jax.numpy as jnp
from jax import lax
from jax.experimental import pallas as pl
from jax.experimental.pallas import tpu as pltpu
from jax.sharding import PartitionSpec as P

HEADS = 8
WT = 8
HALF = WT // 2
AXES = ("frame", "clip")
BIG = 2.0**100
UNROLL = 8
EXT = 16
f32, bf16 = jnp.float32, jnp.bfloat16


def swapped(array, odd):
    devices = lax.axis_size("frame")
    pairs = [(i, (((i + odd) ^ 1) - odd) % devices) for i in range(devices)]
    return lax.ppermute(array, "frame", pairs)


def mm(a, b, ca=1, cb=0):
    return lax.dot_general(a, b, (((ca,), (cb,)), ((), ())), preferred_element_type=f32)


def role(place, odd, frames):
    first = lax.rem(place, 2) == odd
    own_start = jnp.where(first, HALF, 0)
    win = jnp.where(first, 0, 1)
    return first, own_start, win


def pick_kernel(tok, gr, out):
    _, start, win = role(lax.axis_index("frame"), 1, tok.shape[0])
    for k in range(HALF):
        out[0, k] = tok[start + k, 1 - win]
        out[1, k] = gr[start + k, 1 - win]


def block_kernel(
    frame_total, last, lengths, tok, gr, halo, gain, nb, w32, wp32, bq, bp, *refs
):
    if last:
        acc_in, mixed, gtok, send, pay = refs[:5]
    else:
        mixed, gtok, send, acc_out = refs[:4]
    xs, gs, normT, gN, qkvT, doT, attT, dqT, acc, ext, w, wp = refs[-12:]
    acc = acc if last else acc_out
    w[...] = w32[...].astype(bf16)
    wp[...] = wp32[...].astype(bf16)
    patch, width = tok.shape[2:]
    rows = WT * patch
    depth = width // HEADS
    scale = depth ** (-0.5)
    length = lengths[0]
    frames = tok.shape[0]
    place = lax.axis_index("frame")
    first, own_start, win = role(place, int(last), frames)
    own_frame = place * frames + own_start
    halo_frame = place * frames + jnp.where(first, frames, -HALF)
    halo_frame = jnp.where(halo_frame < 0, halo_frame + frame_total, halo_frame)
    halo_frame = jnp.where(halo_frame >= frame_total, halo_frame - frame_total, halo_frame)

    def valid_of(u):
        t = own_frame + u if u < HALF else halo_frame + (u - HALF)
        return jnp.where(t < length, 1.0, 0.0).astype(f32)

    for u in range(WT):
        at = pl.ds(u * patch, patch)
        k = u % HALF
        if u < HALF:
            x_u, g_u = tok[own_start + k, win], gr[own_start + k, win]
        else:
            x_u, g_u = halo[0, k], halo[1, k]
        xs[at, :] = x_u.astype(f32)
        gs[at, :] = g_u.astype(f32) * valid_of(u)

    lane = lax.broadcasted_iota(jnp.int32, (EXT, rows), 1)
    row = lax.broadcasted_iota(jnp.int32, (EXT, rows), 0)
    u_lane = jnp.zeros((EXT, rows), jnp.int32)
    for u in range(1, WT):
        u_lane = u_lane + jnp.where(lane >= u * patch, 1, 0)
    t_lane = jnp.where(u_lane < HALF, own_frame + u_lane, halo_frame + u_lane - HALF)
    bad = jnp.where(t_lane < length, 0.0, 1.0)
    reg = jnp.where(t_lane < HALF, 1.0, 0.0)
    q_rows = jnp.where(row == 1, reg, jnp.where(row == 2, 1.0 - reg, 0.0))
    k_rows = jnp.where(row == 1, 1.0 - reg, jnp.where(row == 2, reg, 0.0))
    ext[0] = jnp.where(row == 0, 1.0, q_rows).astype(bf16)
    ext[1] = (jnp.where(row == 0, bad, k_rows) * -BIG).astype(bf16)
    one_row = jnp.where(row == 0, 1.0, 0.0).astype(bf16)
    two_rows = jnp.where(row < 2, 1.0, 0.0).astype(bf16)

    bqT = jnp.transpose(jnp.broadcast_to(bq[...], (rows, bq.shape[1])))
    x = xs[...]
    mean = jnp.mean(x, axis=-1, keepdims=True)
    xc = x - mean
    var = jnp.mean(xc * xc, axis=-1, keepdims=True)
    rstd = lax.rsqrt(var + 1e-05)
    xhat = xc * rstd
    xs[...] = xhat
    normed = xhat * gain[...] + nb[...]
    normT[:width, :] = jnp.transpose(normed).astype(bf16)
    normT[width:, :] = one_row
    attT[width:, :] = one_row
    qkvT[...] = (mm(w[...], normT[:width, :], 0, 0) + bqT).astype(bf16)
    gN[...] = gs[...].astype(bf16)
    doT[...] = mm(wp[...], gN[...], 1, 1).astype(bf16)

    def head(h):
        at = pl.ds(pl.multiple_of(h * depth, depth), depth)
        at_k = pl.ds(pl.multiple_of(width + h * depth, depth), depth)
        at_v = pl.ds(pl.multiple_of(2 * width + h * depth, depth), depth)
        qT = qkvT[at, :]
        kT = qkvT[at_k, :]
        vT = qkvT[at_v, :]
        d_oT = doT[at, :]
        sT = mm(jnp.concatenate([kT, ext[1]], 0), jnp.concatenate([qT, ext[0]], 0), 0, 0)
        top = jnp.max(sT, axis=0, keepdims=True)
        e = jnp.exp2((sT - top) * (scale * math.log2(math.e)))
        eb = e.astype(bf16)
        summed = mm(jnp.concatenate([vT, one_row], 0), eb)
        inv = 1.0 / summed[depth : depth + 1]
        oT = (summed[:depth] * inv).astype(bf16)
        attT[at, :] = oT
        d_o = d_oT.astype(f32)
        delta = jnp.sum(d_o * oT.astype(f32), axis=0, keepdims=True) * inv
        d_on = (d_o * inv).astype(bf16)
        hi = delta.astype(bf16).astype(f32)
        lo = delta - hi
        d_ext = jnp.where(row == 0, -hi, jnp.where(row == 1, -lo, 0.0)).astype(bf16)
        dpT = mm(jnp.concatenate([vT, two_rows], 0), jnp.concatenate([d_on, d_ext], 0), 0, 0)
        dsT = (e * dpT).astype(bf16)
        dqT[at_v, :] = mm(d_on, eb, 1, 1).astype(bf16)
        dqT[at, :] = (mm(kT, dsT) * scale).astype(bf16)
        dqT[at_k, :] = (mm(qT, dsT, 1, 1) * scale).astype(bf16)

    def heads(i, carry):
        for k in range(UNROLL):
            head(i * UNROLL + k)
        return carry

    lax.fori_loop(0, HEADS // UNROLL, heads, 0)

    wide = 3 * width
    acc[: width + EXT, :wide] = mm(normT[...], dqT[...], 1, 1)
    acc[: width + EXT, wide:] = mm(attT[...], gN[...])
    gs[...] = jnp.transpose(mm(wp[...], attT[:width, :], 0, 0)) + bp[...]
    for u in range(WT):
        k = u % HALF
        b_u = (gs[pl.ds(u * patch, patch), :] * valid_of(u)).astype(bf16)
        if u < HALF:
            x_u = tok[own_start + k, win].astype(f32)
            mixed[k] = (x_u + b_u.astype(f32)).astype(bf16)
        else:
            send[0, k] = b_u
    dn = jnp.transpose(mm(w[...], dqT[...]).astype(bf16).astype(f32))
    xhat = xs[...]
    small = width + EXT
    acc[small : small + 1, :width] = jnp.sum(dn * xhat, axis=0, keepdims=True)
    acc[small : small + 1, width : 2 * width] = jnp.sum(dn, axis=0, keepdims=True)
    acc[small : small + 1, 2 * width :] = jnp.zeros((1, 2 * width), f32)
    acc[small + 1 :, :] = jnp.zeros((EXT - 1, 4 * width), f32)
    dxh = dn * gain[...]
    m1 = jnp.mean(dxh, axis=-1, keepdims=True)
    m2 = jnp.mean(dxh * xhat, axis=-1, keepdims=True)
    gs[...] = rstd * (dxh - m1 - xhat * m2)
    for u in range(WT):
        k = u % HALF
        d_u = gs[pl.ds(u * patch, patch), :].astype(bf16)
        if u < HALF:
            g_u = gr[own_start + k, win].astype(f32)
            gtok[k] = (g_u + d_u.astype(f32)).astype(bf16)
        else:
            send[1, k] = d_u
    if last:
        chunks, deep, lanes = pay.shape
        across = 4 * width // lanes
        for c in range(chunks):
            r, k = c // across, c % across
            at = (slice(r * deep, (r + 1) * deep), slice(k * lanes, (k + 1) * lanes))
            pay[c] = (acc_in[at] + acc[at]).astype(bf16)


def join_kernel(tok, gr, mixed1, gtok1, back1, mixed2, gtok2, back2, mixed, gtok):
    for n, (m, g, back) in enumerate(((mixed1, gtok1, back1), (mixed2, gtok2, back2))):
        _, start, win = role(lax.axis_index("frame"), n, tok.shape[0])
        other, other_win = start, 1 - win
        for k in range(HALF):
            mixed[start + k, win] = m[k]
            gtok[start + k, win] = g[k]
            at = other + k
            mixed[at, other_win] = (
                tok[at, other_win].astype(f32) + back[0, k].astype(f32)
            ).astype(bf16)
            gtok[at, other_win] = (
                gr[at, other_win].astype(f32) + back[1, k].astype(f32)
            ).astype(bf16)


def spread_kernel(parts, out):
    total = parts[0].astype(f32)
    for k in range(1, parts.shape[0]):
        total = total + parts[k].astype(f32)
    total = total.astype(bf16)
    for k in range(out.shape[0]):
        out[k] = total


def spread(parts, copies):
    vmem = pl.BlockSpec(memory_space=pltpu.VMEM)
    return pl.pallas_call(
        spread_kernel,
        name="spread",
        out_shape=jax.ShapeDtypeStruct((copies,) + parts.shape[1:], bf16),
        in_specs=[vmem],
        out_specs=vmem,
        compiler_params=pltpu.CompilerParams(vmem_limit_bytes=8 << 20),
    )(parts)


def unpack_kernel(width, got, dgain, dnb, dwq, dbq, dwp, dbp, full):
    chunks, deep, lanes = got.shape
    across = 4 * width // lanes
    for c in range(chunks):
        top, k = c // across * deep, c % across
        block = got[c].astype(f32)
        n = min(deep, width - top)
        cols = slice(k * lanes, (k + 1) * lanes)
        if k * lanes < 3 * width:
            dwq[top : top + n, cols] = block[:n]
        else:
            dwp[top : top + n, k * lanes - 3 * width : (k + 1) * lanes - 3 * width] = block[:n]
        for m, row in enumerate((width, width + EXT)):
            if top <= row < top + deep:
                full[m : m + 1, cols] = block[row - top : row - top + 1]
    dbq[...] = full[0, : 3 * width]
    dbp[...] = full[0, 3 * width :]
    dgain[...] = full[1, :width]
    dnb[...] = full[1, width : 2 * width]


def groups_of(bits, devices):
    offsets = []
    for m in range(1 << len(bits)):
        offsets.append(sum(1 << b for k, b in enumerate(bits) if m >> k & 1))
    mask = sum(1 << b for b in bits)
    return [[base | o for o in offsets] for base in range(devices) if not base & mask]


def exchange(x, bits):
    devices = lax.axis_size(AXES)
    return lax.all_to_all(
        x, AXES, 0, 0, tiled=True, axis_index_groups=groups_of(bits, devices)
    )


NEAR = (0, 1, 5, 6, 7)
ALONG_Z = (2, 3, 4)


def per_device(
    tokens, lengths, norm_gain, norm_bias, qkv_weight, qkv_bias, proj_weight, proj_bias, grad_out
):
    _, frames, windows, patch, width = tokens.shape
    rows = WT * patch
    frame_total = frames * lax.axis_size("frame")
    place = lax.axis_index("frame")
    tok, gr = tokens[0], grad_out[0]
    vmem = pl.BlockSpec(memory_space=pltpu.VMEM)
    smem = pl.BlockSpec(memory_space=pltpu.SMEM)
    half = jax.ShapeDtypeStruct((HALF, patch, width), bf16)
    halves = jax.ShapeDtypeStruct((2, HALF, patch, width), bf16)

    _, own_start, win = role(place, 0, frames)
    size = (1, HALF, 1, patch, width)
    at = (0, own_start, 1 - win, 0, 0)
    give1 = jnp.concatenate(
        [lax.dynamic_slice(a, at, size)[0, :, 0][None] for a in (tokens, grad_out)]
    )
    halo1 = swapped(give1, 0)
    give2 = pl.pallas_call(
        pick_kernel,
        name="pick",
        out_shape=halves,
        in_specs=[vmem] * 2,
        out_specs=vmem,
        compiler_params=pltpu.CompilerParams(vmem_limit_bytes=8 << 20),
    )(tok, gr)
    halo2 = swapped(give2, 1)
    near = 1 << len(NEAR)
    deep = (width + 2 * EXT) * 4 * width // 128 // near
    total_rows = width + 2 * EXT
    sums_type = jax.ShapeDtypeStruct((total_rows, 4 * width), f32)
    pay_type = jax.ShapeDtypeStruct((near, deep, 128), bf16)

    def block(last, halo, *more):
        return pl.pallas_call(
            functools.partial(block_kernel, frame_total, last),
            name="second_window" if last else "first_window",
            out_shape=(half, half, halves, pay_type if last else sums_type),
            in_specs=[smem] + [vmem] * (9 + len(more)),
            out_specs=(vmem,) * 4,
            scratch_shapes=[
                pltpu.VMEM((rows, width), f32),
                pltpu.VMEM((rows, width), f32),
                pltpu.VMEM((width + EXT, rows), bf16),
                pltpu.VMEM((rows, width), bf16),
                pltpu.VMEM((3 * width, rows), bf16),
                pltpu.VMEM((width, rows), bf16),
                pltpu.VMEM((width + EXT, rows), bf16),
                pltpu.VMEM((3 * width, rows), bf16),
                pltpu.VMEM((total_rows, 4 * width), f32),
                pltpu.VMEM((2, EXT, rows), bf16),
                pltpu.VMEM((width, 3 * width), bf16),
                pltpu.VMEM((width, width), bf16),
            ],
            compiler_params=pltpu.CompilerParams(vmem_limit_bytes=32 << 20),
            cost_estimate=pl.CostEstimate(
                flops=8_000_000_000, bytes_accessed=8_000_000, transcendentals=2_000_000
            ),
        )(
            lengths, tok, gr, halo, norm_gain[None], norm_bias[None], qkv_weight,
            proj_weight, qkv_bias[None], proj_bias[None], *more,
        )

    mixed1, gtok1, send1, sums1 = block(False, halo1)
    back1 = swapped(send1, 0)
    mixed2, gtok2, send2, pay = block(True, halo2, sums1)
    pay, back1 = lax.optimization_barrier((pay, back1))
    back2 = swapped(send2, 1)
    part = spread(exchange(pay, NEAR), 1 << len(ALONG_Z))
    total = spread(exchange(part, ALONG_Z), near)
    got = exchange(total, NEAR)
    slab = jax.ShapeDtypeStruct(tok.shape, bf16)
    mixed, gtok = pl.pallas_call(
        join_kernel,
        name="join",
        out_shape=(slab, slab),
        in_specs=[vmem] * 8,
        out_specs=(vmem,) * 2,
        compiler_params=pltpu.CompilerParams(vmem_limit_bytes=16 << 20),
        cost_estimate=pl.CostEstimate(
            flops=20_000_000_000, bytes_accessed=4_000_000, transcendentals=0
        ),
    )(
        tok, gr,
        mixed1, gtok1, back1, mixed2, gtok2, back2,
    )
    dgain, dnb, dwq, dbq, dwp, dbp = pl.pallas_call(
        functools.partial(unpack_kernel, width),
        name="unpack",
        out_shape=(
            jax.ShapeDtypeStruct((width,), f32),
            jax.ShapeDtypeStruct((width,), f32),
            jax.ShapeDtypeStruct((width, 3 * width), f32),
            jax.ShapeDtypeStruct((3 * width,), f32),
            jax.ShapeDtypeStruct((width, width), f32),
            jax.ShapeDtypeStruct((width,), f32),
        ),
        in_specs=[vmem],
        out_specs=(vmem,) * 6,
        scratch_shapes=[pltpu.VMEM((2, 4 * width), f32)],
        compiler_params=pltpu.CompilerParams(vmem_limit_bytes=16 << 20),
    )(got)
    return (mixed[None], gtok[None], dgain, dnb, dwq, dbq, dwp, dbp)


def solution(mesh):
    split = P("clip", "frame", None, None, None)
    in_specs = (split, P("clip"), P(), P(), P(), P(), P(), P(), split)
    out_specs = (split, split, P(), P(), P(), P(), P(), P())
    return jax.shard_map(
        per_device, mesh=mesh, in_specs=in_specs, out_specs=out_specs, check_vma=False
    )
```
